32 devices in a mesh: groups: 2 (over y), hid: 2 (over x), exp: 4 (over z), pair: 2 (over core).
Axes of the slice: x: 2, y: 2, z: 4, core: 2. Of those that a mesh axis runs over, the one named last changes fastest.
Arguments:
- queries: bfloat16 [8, 8, 2048], P(('groups', 'exp'), ('hid', 'pair')), parts along dimension 0, may hold values from -800 to 800
- keys_cache: bfloat16 [8, 2048, 512], P(('groups', 'exp'), ('hid', 'pair')), parts along dimension 0, may hold values from -6 to 6
- values_cache: bfloat16 [8, 2048, 512], P(('groups', 'exp'), ('hid', 'pair')), parts along dimension 0, may hold values from -6 to 6
- span_keys: bfloat16 [8, 8, 512], P(('groups', 'exp'), ('hid', 'pair')), parts along dimension 0, may hold values from -6 to 6
- span_values: bfloat16 [8, 8, 512], P(('groups', 'exp'), ('hid', 'pair')), parts along dimension 0, may hold values from -6 to 6
- cached: int32 [8], P(('groups', 'exp')), parts along dimension 0, may hold values from 512 to 2048, as said below
- residual: bfloat16 [8, 8, 2048], P(('groups', 'exp'), ('hid', 'pair')), parts along dimension 0, may hold values from -200 to 200
- norm_gain: float32 [2048], replicated, may hold values from 0.1 to 1.9
- routes: int32 [8, 8, 2], P(('groups', 'exp'), ('hid', 'pair')), parts along dimension 0, may hold values from 0 to 3, all different within a row; in each aligned block of 2 rows (0 to 1, 2 to 3, ..., all dimensions but the last counted through in order) at most 2 rows name the same one
- route_scores: float32 [8, 8, 2], P(('groups', 'exp'), ('hid', 'pair')), parts along dimension 0, may hold values from 0.1 to 1
- w_gate: bfloat16 [4, 2048, 8192], P('exp', None, ('hid', 'pair')), may hold values from -0.125 to 0.125
- w_up: bfloat16 [4, 2048, 8192], P('exp', None, ('hid', 'pair')), may hold values from -0.125 to 0.125
- w_down: bfloat16 [4, 8192, 2048], P('exp', ('hid', 'pair')), may hold values from -0.0625 to 0.0625
Outputs:
- attn_out: bfloat16 [8, 8, 2048], P(('groups', 'exp'), ('hid', 'pair')), parts along dimension 0
- moe_out: bfloat16 [8, 8, 2048], P(('groups', 'exp'), ('hid', 'pair')), parts along dimension 0
The draws below stay inside these ranges and needn't reach their ends.
There are 2 independent parts, one for each index of `groups`. The reference program is written for one: setup_inputs(seed, part) draws one part's arguments, and reference() takes and returns one part's arrays. A program takes and returns all parts, laid end to end along the dimension named above; an argument that names none is the same for every part. Nothing has to cross between parts.
Inputs may be any that keep to these rules, and one draw needn't show every extreme that they name: `routes`: in the 2 rows of one device, taken in order, no expert is named by more than 2 rows, and some device's rows reach 2. The longest request of a part has exactly 2048 cached positions; cache positions at or past a request's cached length hold no keys of that request.
All inputs are finite; a program needn't handle non-finite values.
Results may differ from the reference program's by a relative error of at most 0.007.
Values may be sent and summed in bfloat16 or wider, within the bound.
No kernel may reach another device: no remote copies, remote signals or barrier semaphores. Data moves between devices by JAX's collectives and lax.ppermute only.
A program may use at most 128 MiB of HBM per device.

```python
import math
import jax
import jax.numpy as jnp
import numpy as np
from jax import lax

D = 2048
FF = 8192
HEADS = 16
KV_HEADS = 4
HEAD_DIM = 128
TOK_DEV = 2
EXPERTS = 4
REQS = 4
SPAN = 8
CACHE = 2048
CAP = 2


def common_attention(key):
    query_key = jax.random.fold_in(key, 11)
    cache_key = jax.random.fold_in(key, 12)
    query_draw = 1.5 * jax.random.truncated_normal(query_key, -4.0, 4.0, (REQS, SPAN, HEADS, HEAD_DIM), jnp.float32)
    cache_keys = jax.random.truncated_normal(cache_key, -6.0, 6.0, (REQS, CACHE, KV_HEADS, HEAD_DIM), jnp.float32)
    return (query_draw, cache_keys)


def draw_queries(key, part):
    query_draw, cache_keys = common_attention(key)
    return query_draw.reshape(REQS, SPAN, HEADS * HEAD_DIM).astype(jnp.bfloat16)


def draw_keys_cache(key, part):
    query_draw, cache_keys = common_attention(key)
    return cache_keys.reshape(REQS, CACHE, KV_HEADS * HEAD_DIM).astype(jnp.bfloat16)


def draw_cached(key, part):
    lengths = jax.random.randint(jax.random.fold_in(key, 21), (REQS,), CACHE // 4, CACHE + 1)
    longest = jax.random.randint(jax.random.fold_in(key, 22), (), 0, REQS)
    return lengths.at[longest].set(CACHE).astype(jnp.int32)


def draw_residual(key, part):
    normal_part = jax.random.truncated_normal(jax.random.fold_in(key, 31), -6.0, 6.0, (REQS, SPAN, D), jnp.float32)
    row_scale = jnp.exp(jax.random.uniform(jax.random.fold_in(key, 32), (REQS, SPAN, 1), jnp.float32, 0.0, 2.302585))
    column_scale = jnp.exp(jax.random.uniform(jax.random.fold_in(key, 33), (1, 1, D), jnp.float32, 0.0, 2.302585))
    values = 0.25 * normal_part * row_scale * column_scale
    return values.astype(jnp.bfloat16)


def block_levels(stream_key, extent, pieces, least, high):
    level = 1.0
    for axis_at, parts in pieces:
        steps = jax.random.uniform(jax.random.fold_in(jax.random.fold_in(stream_key, 6), axis_at), (parts,), jnp.float32, least / len(pieces), high / len(pieces))
        level = level * jnp.repeat(jnp.exp(steps), extent[axis_at] // parts).reshape((-1,) + (1,) * (len(extent) - 1 - axis_at))
    return level


def shared_out(own_key, own, number, rows, count, top, reach, slope):
    ranking = jax.random.permutation(own_key, count)
    crowded, ordinary = load_shares(count, rows * top, reach, slope, True), load_shares(count, rows * top, reach, slope, False)
    places = jnp.arange(count)

    def named(sizes, rotation):
        used = int((sizes > 0).sum())
        fixed = max(1, used // 4)
        shifted = fixed + (places - fixed + rotation * (used - fixed)) % max(1, count - fixed)
        return jnp.zeros((count,), jnp.int32).at[ranking[jnp.where(places < fixed, places, shifted)]].set(jnp.asarray(sizes, jnp.int32))

    sizes = jnp.where(number % 4 == 0, named(crowded, number // 4), named(ordinary, number - number // 4 - 1))
    mixed = jax.random.permutation(jax.random.fold_in(own, 3), count)
    donor, receiver = mixed[0:count // 2 * 2:2], mixed[1:count // 2 * 2:2]
    slack = jnp.minimum(sizes[donor] - 1, reach - sizes[receiver]) // 2
    slack = jnp.where((donor == ranking[0]) | (receiver == ranking[0]) | (sizes[receiver] == 0), 0, jnp.maximum(slack, 0))
    shifted = jax.random.randint(jax.random.fold_in(own, 4), (count // 2,), 0, 1 << 20) % (slack + 1)
    sizes = sizes.at[donor].add(-shifted).at[receiver].add(shifted)
    items = jnp.searchsorted(jnp.cumsum(sizes), jnp.arange(rows * top), side="right").astype(jnp.int32)
    table = items.reshape(top, rows).T
    table = table[jax.random.permutation(jax.random.fold_in(own, 1), rows)]
    rotation = jax.random.randint(jax.random.fold_in(own, 2), (rows, 1), 0, top)
    return jnp.take_along_axis(table, (jnp.arange(top)[None, :] + rotation) % top, axis=1)


def load_shares(number_of, total, limit, lean, full):
    loads = [(1 << 20) // math.isqrt(grade ** lean) + 1 for grade in range(1, number_of + 1)]
    largest = limit if full else min(limit, max(-(-total // number_of), total * loads[0] // sum(loads)))
    least = 1 if total - largest >= number_of - 1 else 0
    counts, spare = [largest] + [least] * (number_of - 1), total - largest - least * (number_of - 1)
    while spare > 0:
        movable = [i for i in range(1, number_of) if counts[i] < largest] or [i for i in range(1, number_of) if counts[i] < limit]
        mass, remaining = sum([loads[i] for i in movable]), spare
        for i in movable:
            addition = min(limit - counts[i], max(1, remaining * loads[i] // mass), spare)
            counts[i] = counts[i] + addition
            spare = spare - addition
    return np.array(counts)


def centred(stream_key, extent, spread, limit, cuts=(), held_as=jnp.bfloat16):
    level = block_levels(stream_key, extent, cuts, -0.22, 0.18) if cuts else 1.0
    result = jax.random.normal(stream_key, extent, jnp.float32) * spread * level
    return jnp.minimum(jnp.maximum(result, -limit), limit).astype(held_as)


def setup_inputs(seed: int = 0, part: int = 0) -> dict:
    splits = jax.random.split(jax.random.key(seed), 14)
    part_keys = jax.random.split(jax.random.fold_in(splits[13], part), 14)
    queries = draw_queries(jax.random.fold_in(jax.random.fold_in(splits[13], part), 71), part)
    keys_cache = draw_keys_cache(jax.random.fold_in(jax.random.fold_in(splits[13], part), 71), part)
    values_cache = centred(part_keys[2], (REQS, CACHE, KV_HEADS * HEAD_DIM), 1.0, 6.0, ((0, 4), (1, 4)))
    span_keys = centred(part_keys[3], (REQS, SPAN, KV_HEADS * HEAD_DIM), 1.0, 6.0, ((0, 4), (1, 4)))
    span_values = centred(part_keys[4], (REQS, SPAN, KV_HEADS * HEAD_DIM), 1.0, 6.0, ((0, 4), (1, 4)))
    cached = draw_cached(jax.random.fold_in(jax.random.fold_in(splits[13], part), 71), part)
    residual = draw_residual(jax.random.fold_in(jax.random.fold_in(splits[13], part), 71), part)
    norm_gain = jnp.clip(1.0 + 0.18 * jax.random.normal(splits[7], (D,), jnp.float32), 0.1, 1.9)
    routes_keys = jax.random.split(jax.random.fold_in(part_keys[8], 1), REQS * SPAN // TOK_DEV)
    routes_turns = jax.random.permutation(jax.random.fold_in(part_keys[8], 3), REQS * SPAN // TOK_DEV)
    routes = jax.vmap(lambda own, number: shared_out(jax.random.fold_in(part_keys[8], 2), own, number, TOK_DEV, EXPERTS, 2, CAP, 2))(routes_keys, routes_turns).reshape((REQS, SPAN, 2))
    route_scores = jnp.clip(jnp.exp(math.log(1.0) - 2.3025851 * jax.random.uniform(part_keys[9], (REQS, SPAN, 2), jnp.float32) ** block_levels(part_keys[9], (REQS, SPAN, 2), ((0, 4), (1, 4)), -0.2, 0.2)), 0.1, 1.0)
    w_gate = centred(splits[10], (EXPERTS, D, FF), D ** -0.5, 0.125, ((0, 4), (2, 4)))
    w_up = centred(splits[11], (EXPERTS, D, FF), D ** -0.5, 0.125, ((0, 4), (2, 4)))
    w_down = centred(splits[12], (EXPERTS, FF, D), FF ** -0.5, 0.0625, ((0, 4), (1, 4)))
    return dict(queries=queries, keys_cache=keys_cache, values_cache=values_cache, span_keys=span_keys, span_values=span_values, cached=cached, residual=residual, norm_gain=norm_gain, routes=routes, route_scores=route_scores, w_gate=w_gate, w_up=w_up, w_down=w_down)


masked_score = -1e+30
norm_epsilon = 1e-05

def attend_request(packed):
    query_block, key_block, value_block, new_keys, new_values, cached_len = packed
    span_rows = query_block.shape[0]
    head_group = HEADS // KV_HEADS
    all_keys = jnp.concatenate([key_block, new_keys], axis=0).astype(jnp.float32)
    all_values = jnp.concatenate([value_block, new_values], axis=0).astype(jnp.float32)
    key_heads = all_keys.reshape(CACHE + span_rows, KV_HEADS, HEAD_DIM)
    value_heads = all_values.reshape(CACHE + span_rows, KV_HEADS, HEAD_DIM)
    grouped = query_block.astype(jnp.float32).reshape(span_rows, KV_HEADS, head_group, HEAD_DIM)
    scores = jnp.einsum('rgqd,ngd->gqrn', grouped, key_heads) * HEAD_DIM ** (-0.5)
    key_position = jnp.arange(CACHE + span_rows, dtype=jnp.int32)
    row_index = jnp.arange(span_rows, dtype=jnp.int32)
    cache_seen = (key_position < CACHE) & (key_position < cached_len)
    span_seen = (key_position[None, :] >= CACHE) & (key_position[None, :] - CACHE <= row_index[:, None])
    allowed = cache_seen[None, :] | span_seen
    scores = jnp.where(allowed, scores, masked_score)
    row_max = lax.optimization_barrier(jnp.max(scores, axis=3, keepdims=True))
    weights = jnp.where(allowed, jnp.exp(scores - row_max), 0.0)
    totals = lax.optimization_barrier(jnp.sum(weights, axis=3))
    numerator = jnp.einsum('gqrn,ngd->rgqd', weights, value_heads, precision=lax.Precision.HIGHEST)
    normalizer = jnp.transpose(totals, (2, 0, 1))[..., None]
    return (numerator / normalizer).reshape(span_rows, HEADS * HEAD_DIM).astype(jnp.bfloat16)

def expert_apply(packed):
    rows_in, gate_weight, up_weight, down_weight = packed
    gate_part = jnp.dot(rows_in, gate_weight, preferred_element_type=jnp.float32)
    up_part = jnp.dot(rows_in, up_weight, preferred_element_type=jnp.float32)
    hidden = (jax.nn.silu(gate_part) * up_part).astype(jnp.bfloat16)
    return jnp.dot(hidden, down_weight, preferred_element_type=jnp.float32).astype(jnp.bfloat16)

def reference(queries, keys_cache, values_cache, span_keys, span_values, cached, residual, norm_gain, routes, route_scores, w_gate, w_up, w_down):
    attn_out = lax.map(attend_request, (queries, keys_cache, values_cache, span_keys, span_values, cached))
    token_total = REQS * SPAN
    mixed = residual.reshape(token_total, D).astype(jnp.float32) + attn_out.reshape(token_total, D).astype(jnp.float32)
    mean_square = lax.optimization_barrier(jnp.mean(mixed * mixed, axis=1, keepdims=True))
    normed = (mixed * lax.rsqrt(mean_square + norm_epsilon) * norm_gain).astype(jnp.bfloat16)
    pair_scores = route_scores.reshape(token_total, 2)
    route_weight = pair_scores / lax.optimization_barrier(jnp.sum(pair_scores, axis=1, keepdims=True))
    chosen = routes.reshape(token_total * 2).astype(jnp.int32)
    block_count = token_total // TOK_DEV
    one_hot = (chosen[:, None] == jnp.arange(EXPERTS, dtype=jnp.int32)[None, :]).astype(jnp.int32)
    blocked = one_hot.reshape(block_count, 2 * TOK_DEV, EXPERTS)
    earlier = (jnp.cumsum(blocked, axis=1) - blocked).reshape(token_total * 2, EXPERTS)
    slot_index = lax.optimization_barrier(jnp.sum(earlier * one_hot, axis=1)).astype(jnp.int32)
    token_of = (jnp.arange(token_total * 2, dtype=jnp.int32) // 2).astype(jnp.int32)
    block_of = (token_of // TOK_DEV).astype(jnp.int32)
    column = (block_of * CAP + slot_index).astype(jnp.int32)
    table = jnp.zeros((EXPERTS, block_count * CAP), jnp.int32).at[chosen, column].set(token_of)
    expert_inputs = jnp.take(normed, table.reshape(-1), axis=0).reshape(EXPERTS, block_count * CAP, D)
    results = lax.map(expert_apply, (expert_inputs, w_gate, w_up, w_down))
    picked = results[chosen, column].astype(jnp.float32).reshape(token_total, 2, D)
    moe_out = lax.optimization_barrier(jnp.sum(picked * route_weight[:, :, None], axis=1)).astype(jnp.bfloat16)
    return (attn_out, moe_out.reshape(REQS, SPAN, D))
```

```python
import functools

import jax
import jax.numpy as jnp
from jax import lax
from jax.experimental import pallas as pl
from jax.experimental.pallas import tpu as pltpu
from jax.sharding import PartitionSpec as P

HEAD_DIM = 128
SEQ = ("hid", "pair")

masked_score = -1e30
norm_epsilon = 1e-05


def partners(value, axes, count):
    return [value[0]] + [
        lax.ppermute(value[k], axes, [(i, i ^ k) for i in range(count)]) for k in range(1, count)
    ]


def split_two(x):
    high = x.astype(jnp.bfloat16).astype(jnp.float32)
    low = (x - high).astype(jnp.bfloat16).astype(jnp.float32)
    return high, low


def attend_kernel(count, *refs):
    query_refs, refs = refs[:count], refs[count:]
    cached_ref, key_ref, value_ref, new_key_ref, new_value_ref, residual_ref, out_ref, rows_ref = refs
    token_dev, width = query_refs[0].shape
    row_count = count * token_dev
    cache_dev = key_ref.shape[0]
    key_heads = key_ref.shape[1] // HEAD_DIM
    heads = width // HEAD_DIM
    per_group = heads // key_heads
    own = lax.axis_index(SEQ)
    scale = HEAD_DIM ** (-0.5)
    for k in range(count):
        rows_ref[k * token_dev : (k + 1) * token_dev, :] = query_refs[k][...].astype(jnp.float32)
    group_rows = per_group * row_count
    position = own * cache_dev + lax.broadcasted_iota(jnp.int32, (1, cache_dev), 1)
    seen = position < cached_ref[0]
    index = lax.broadcasted_iota(jnp.int32, (group_rows, 1), 0) % row_count
    row_index = (own ^ (index // token_dev)) * token_dev + index % token_dev
    lane = lax.broadcasted_iota(jnp.int32, (group_rows, HEAD_DIM), 1)
    stats = jnp.zeros((group_rows, HEAD_DIM), jnp.float32)
    for g in range(key_heads):
        span = slice(g * HEAD_DIM, (g + 1) * HEAD_DIM)
        rows = jnp.concatenate(
            [
                rows_ref[:, h * HEAD_DIM : (h + 1) * HEAD_DIM]
                for h in range(g * per_group, (g + 1) * per_group)
            ],
            axis=0,
        )
        scores = lax.dot_general(
            rows.astype(jnp.bfloat16),
            key_ref[:, span],
            (((1,), (1,)), ((), ())),
            preferred_element_type=jnp.float32,
        )
        scores = jnp.where(seen, scores * scale, masked_score)
        row_max = jnp.max(scores, axis=1, keepdims=True)
        new_scores = []
        for t in range(token_dev):
            new_key = new_key_ref[t : t + 1, span].astype(jnp.float32)
            score = jnp.sum(rows * new_key, axis=1, keepdims=True) * scale
            allowed = own * token_dev + t <= row_index
            score = jnp.where(allowed, score, masked_score)
            row_max = jnp.maximum(row_max, score)
            new_scores.append((score, allowed))
        max_high, max_low = split_two(row_max)
        row_max = max_high + max_low
        weights = jnp.where(seen, jnp.exp(scores - row_max), 0.0)
        total = jnp.sum(weights, axis=1, keepdims=True)
        weights_high = weights.astype(jnp.bfloat16)
        weights_low = (weights - weights_high.astype(jnp.float32)).astype(jnp.bfloat16)
        values = value_ref[:, span]
        sums = jnp.dot(weights_high, values, preferred_element_type=jnp.float32)
        sums = sums + jnp.dot(weights_low, values, preferred_element_type=jnp.float32)
        for t in range(token_dev):
            score, allowed = new_scores[t]
            weight = jnp.where(allowed, jnp.exp(score - row_max), 0.0)
            total = total + weight
            sums = sums + weight * new_value_ref[t : t + 1, span].astype(jnp.float32)
        total_high, total_low = split_two(total)
        for at, column in enumerate((max_high, max_low, total_high, total_low)):
            stats = jnp.where(lane == 4 * g + at, column, stats)
        out_ref[g * group_rows : (g + 1) * group_rows, :] = sums.astype(jnp.bfloat16)
    first = heads * row_count
    out_ref[first : first + group_rows, :] = stats.astype(jnp.bfloat16)
    first = first + group_rows
    out_ref[first:, :] = residual_ref[...]


def stage_kernel(residual_ref, out_ref, rows_ref):
    token_dev = residual_ref.shape[0]
    for h in range(out_ref.shape[0] // token_dev):
        rows_ref[h * token_dev : (h + 1) * token_dev, :] = residual_ref[
            :, h * HEAD_DIM : (h + 1) * HEAD_DIM
        ].astype(jnp.float32)
    out_ref[...] = rows_ref[...].astype(jnp.bfloat16)


def merge_kernel(count, token_dev, key_heads, *refs):
    part_refs, (gain_ref, attn_ref, normed_ref) = refs[:count], refs[count:]
    row_count, width = normed_ref.shape
    heads = width // HEAD_DIM
    per_group = heads // key_heads
    group_rows = per_group * row_count
    stats_first = heads * row_count
    res_first = stats_first + group_rows
    res_rows = heads * token_dev
    from_row = lax.broadcasted_iota(jnp.int32, (group_rows, group_rows), 1)
    to_row = lax.broadcasted_iota(jnp.int32, (group_rows, group_rows), 0)
    swaps = [(from_row == (to_row ^ (k * token_dev))).astype(jnp.bfloat16) for k in range(count)]

    def reordered(k, first):
        part = part_refs[k][first : first + group_rows, :]
        if k == 0:
            return part.astype(jnp.float32)
        return jnp.dot(swaps[k], part, preferred_element_type=jnp.float32)

    stats = [reordered(k, stats_first) for k in range(count)]
    per_head = lax.broadcasted_iota(jnp.int32, (group_rows, res_rows), 0)
    res_from = lax.broadcasted_iota(jnp.int32, (group_rows, res_rows), 1)
    res_head, res_token = res_from // token_dev, res_from % token_dev
    mixed = []
    square = jnp.zeros((row_count, HEAD_DIM), jnp.float32)
    for g in range(key_heads):
        maxima = [s[:, 4 * g : 4 * g + 1] + s[:, 4 * g + 1 : 4 * g + 2] for s in stats]
        totals = [s[:, 4 * g + 2 : 4 * g + 3] + s[:, 4 * g + 3 : 4 * g + 4] for s in stats]
        joint = functools.reduce(jnp.maximum, maxima)
        scales = [jnp.exp(m - joint) for m in maxima]
        total = sum(t * s for t, s in zip(totals, scales))
        sums = sum(reordered(k, g * group_rows) * scales[k] for k in range(count))
        attn = (sums / total).astype(jnp.bfloat16).astype(jnp.float32)
        residual = jnp.zeros((group_rows, HEAD_DIM), jnp.float32)
        for k in range(count):
            row = per_head % row_count
            choose = (
                (res_head == g * per_group + per_head // row_count)
                & (row // token_dev == k)
                & (row % token_dev == res_token)
            )
            residual = residual + jnp.dot(
                choose.astype(jnp.bfloat16),
                part_refs[k][res_first : res_first + res_rows, :],
                preferred_element_type=jnp.float32,
            )
        for i in range(per_group):
            h = g * per_group + i
            tile = attn[i * row_count : (i + 1) * row_count, :]
            attn_ref[:, h * HEAD_DIM : (h + 1) * HEAD_DIM] = tile[:token_dev, :].astype(jnp.bfloat16)
            tile = tile + residual[i * row_count : (i + 1) * row_count, :]
            square = square + tile * tile
            mixed.append(tile)
    mean_square = jnp.sum(square, axis=1, keepdims=True) / width
    factor = lax.rsqrt(mean_square + norm_epsilon)
    for h in range(heads):
        span = slice(h * HEAD_DIM, (h + 1) * HEAD_DIM)
        normed_ref[:, span] = (mixed[h] * factor * gain_ref[:, span]).astype(jnp.bfloat16)


def expert_kernel(count, token_dev, *refs):
    row_refs, refs = refs[:count], refs[count:]
    gate_ref, up_ref, down_ref = refs[:3]
    own_ref, out_refs = refs[3], refs[4:]
    rows = jnp.concatenate([ref[...].astype(jnp.float32) for ref in row_refs], axis=0).astype(jnp.bfloat16)
    total = rows.shape[0]
    block = count * token_dev
    to_row = lax.broadcasted_iota(jnp.int32, (total, total), 0)
    from_row = lax.broadcasted_iota(jnp.int32, (total, total), 1)
    seq, rest = to_row // block, to_row % block
    source = (rest // token_dev) * (total // count) + seq * token_dev + rest % token_dev
    rows = jnp.dot(
        (from_row == source).astype(jnp.bfloat16), rows, preferred_element_type=jnp.float32
    ).astype(jnp.bfloat16)
    gate = jnp.dot(rows, gate_ref[...], preferred_element_type=jnp.float32)
    up = jnp.dot(rows, up_ref[...], preferred_element_type=jnp.float32)
    hidden = (gate / (1.0 + jnp.exp(-gate)) * up).astype(jnp.bfloat16)
    sums = jnp.dot(hidden, down_ref[...], preferred_element_type=jnp.float32)
    own_ref[...] = sums[:block, :]
    for k, ref in enumerate(out_refs, 1):
        ref[...] = sums[k * block : (k + 1) * block, :].astype(jnp.bfloat16)


def reduce_kernel(seq_count, token_dev, *refs):
    part_refs, out_refs = refs[:seq_count], refs[seq_count:]
    sums = part_refs[0][...]
    for ref in part_refs[1:]:
        sums = sums + ref[...].astype(jnp.float32)
    for k, ref in enumerate(out_refs):
        ref[...] = sums[k * token_dev : (k + 1) * token_dev, :].astype(jnp.bfloat16)


def weigh_kernel(count, *refs):
    part_refs, (routes_ref, scores_ref, out_ref) = refs[:count], refs[count:]
    own = lax.axis_index("exp")
    scores = scores_ref[...]
    weight = scores / jnp.sum(scores, axis=1, keepdims=True)
    routes = routes_ref[...]
    total = jnp.zeros(out_ref.shape, jnp.float32)
    for k, ref in enumerate(part_refs):
        factor = jnp.sum(jnp.where(routes == (own ^ k), weight, 0.0), axis=1, keepdims=True)
        total = total + factor * ref[...].astype(jnp.float32)
    out_ref[...] = total.astype(jnp.bfloat16)


def in_vmem(count):
    return [pl.BlockSpec(memory_space=pltpu.VMEM)] * count


def shape(dims, dtype):
    return jax.ShapeDtypeStruct(dims, dtype)


def kernel_params(row_count):
    return pltpu.CompilerParams(vmem_limit_bytes=max(4, row_count // 2) << 20)


def lasting(microseconds):
    return pl.CostEstimate(flops=microseconds * 1_000_000_000, bytes_accessed=0, transcendentals=0)


def held(value):
    return pltpu.with_memory_space_constraint(value, pltpu.VMEM)


def per_device(
    queries,
    keys_cache,
    values_cache,
    span_keys,
    span_values,
    cached,
    residual,
    norm_gain,
    routes,
    route_scores,
    w_gate,
    w_up,
    w_down,
):
    token_dev, width = queries.shape[1:]
    seq_count, exp_count = lax.axis_size(SEQ), lax.axis_size("exp")
    row_count = seq_count * token_dev
    key_heads = keys_cache.shape[2] // HEAD_DIM
    heads = width // HEAD_DIM
    part_rows = heads * row_count + heads // key_heads * row_count + heads * token_dev
    bf16, f32 = jnp.bfloat16, jnp.float32

    all_queries = partners([queries[0]] * seq_count, SEQ, seq_count)
    staged = pl.pallas_call(
        stage_kernel,
        out_shape=shape((heads * token_dev, HEAD_DIM), bf16),
        in_specs=in_vmem(1),
        out_specs=in_vmem(1)[0],
        scratch_shapes=[pltpu.VMEM((heads * token_dev, HEAD_DIM), f32)],
        compiler_params=kernel_params(row_count),
        cost_estimate=lasting(4),
        name="stage",
    )(residual[0])
    part = pl.pallas_call(
        functools.partial(attend_kernel, seq_count),
        out_shape=shape((part_rows, HEAD_DIM), bf16),
        in_specs=in_vmem(seq_count) + [pl.BlockSpec(memory_space=pltpu.SMEM)] + in_vmem(5),
        out_specs=in_vmem(1)[0],
        scratch_shapes=[pltpu.VMEM((row_count, width), f32)],
        compiler_params=kernel_params(row_count),
        cost_estimate=lasting(8),
        name="attend",
    )(
        *all_queries,
        cached,
        held(keys_cache[0]),
        held(values_cache[0]),
        span_keys[0],
        span_values[0],
        staged,
    )
    parts = partners([part] * seq_count, SEQ, seq_count)
    attn_out, normed = pl.pallas_call(
        functools.partial(merge_kernel, seq_count, token_dev, key_heads),
        out_shape=(shape((token_dev, width), bf16), shape((row_count, width), bf16)),
        in_specs=in_vmem(seq_count + 1),
        out_specs=tuple(in_vmem(2)),
        compiler_params=kernel_params(row_count),
        cost_estimate=lasting(8),
        name="merge",
    )(*parts, norm_gain[None])
    rows = partners([normed] * exp_count, "exp", exp_count)
    block = exp_count * token_dev
    sums = pl.pallas_call(
        functools.partial(expert_kernel, exp_count, token_dev),
        out_shape=(shape((block, width), f32),) + (shape((block, width), bf16),) * (seq_count - 1),
        in_specs=in_vmem(exp_count + 3),
        out_specs=tuple(in_vmem(seq_count)),
        compiler_params=kernel_params(row_count),
        name="expert",
    )(*rows, held(w_gate[0]), held(w_up[0]), held(w_down[0]))
    sums = partners(sums, SEQ, seq_count)
    reduced = pl.pallas_call(
        functools.partial(reduce_kernel, seq_count, token_dev),
        out_shape=(shape((token_dev, width), bf16),) * exp_count,
        in_specs=in_vmem(seq_count),
        out_specs=tuple(in_vmem(exp_count)),
        compiler_params=kernel_params(row_count),
        name="reduce",
    )(*sums)
    results = partners(reduced, "exp", exp_count)
    moe_out = pl.pallas_call(
        functools.partial(weigh_kernel, exp_count),
        out_shape=shape((token_dev, width), bf16),
        in_specs=in_vmem(exp_count + 2),
        out_specs=in_vmem(1)[0],
        compiler_params=kernel_params(row_count),
        name="weigh",
    )(*results, routes[0], route_scores[0])
    return (attn_out[None], moe_out[None])


def solution(mesh):
    rows = P(("groups", "exp"), SEQ, None)
    placed = (
        rows,
        rows,
        rows,
        rows,
        rows,
        P(("groups", "exp")),
        rows,
        P(),
        rows,
        rows,
        P("exp", None, SEQ),
        P("exp", None, SEQ),
        P("exp", SEQ, None),
    )
    return jax.shard_map(
        per_device,
        mesh=mesh,
        in_specs=placed,
        out_specs=(rows, rows),
        check_vma=False,
    )
```
